128 devices in a mesh: row: 8 (over x, core), col: 16 (over z, y).
Axes of the slice: x: 4, y: 4, z: 4, core: 2. Of those that a mesh axis runs over, the one named last changes fastest.
Arguments:
- updates: bfloat16 [8, 16, 1280, 4864], P('row', 'col'), may hold values from -0.0390625 to 0.0390625
- map_one: int32 [160], replicated, may hold values from 0 to 223, as said below
- map_two: int32 [112], replicated, may hold values from 0 to 223, as said below
- seeds: int32 [224], replicated, may hold values from 0 to 1073741823
- lower: bfloat16 [16, 16, 10, 128, 512], P('col', None, None, 'row'), may hold values from -0.09375 to 0.09375
Outputs:
- border_samples: float32 [16, 10, 128, 1024], P('col', None, 'row')
The draws below stay inside these ranges and needn't reach their ends.
Inputs may be any that keep to these rules, and one draw needn't show every extreme that they name: `map_one`: for every g, entries g * 10 to (g + 1) * 10 - 1 are strictly increasing and lie in parent tiles g * 14 to (g + 1) * 14 - 1. `map_two`: for every g, entries g * 7 to (g + 1) * 7 - 1 are strictly increasing and lie in parent tiles g * 14 to (g + 1) * 14 - 1.
All inputs are finite; a program needn't handle non-finite values.
Results may differ from the reference program's by a relative error of at most 0.015.
Values may be sent and summed in bfloat16 or wider, within the bound.
No kernel may reach another device: no remote copies, remote signals or barrier semaphores. Data moves between devices by JAX's collectives and lax.ppermute only.
A program may use at most 128 MiB of HBM per device.

```python
import jax
import jax.numpy as jnp
from jax import lax

TILE = 128
SAMPLES = 1024
N1 = 20480
NPIV = 8192
PROWS = 8
PCOLS = 16
ROWS_ONE = 5
ROWS_TWO = 3
T1TILES = 160
T2TILES = 112
PARTILES = 224
PIVTILES = 64
BORDTILES = 160
GROUP1 = 10
GROUP2 = 7
SLOTS1 = 32
SLOTS2 = 38
SLOTS = 38
WINDOW = 14


def window_map(rng_key, groups, per_group, span_tiles):
    scores = jax.random.randint(rng_key, (groups, span_tiles), 0, 1 << 20) * span_tiles + jnp.arange(span_tiles, dtype=jnp.int32)[None, :]
    ranked = jnp.argsort(jnp.argsort(scores, axis=1), axis=1)
    chosen = ranked < per_group
    spots = jnp.arange(span_tiles, dtype=jnp.int32)[None, :]
    ordered = jnp.sort(jnp.where(chosen, spots, spots + span_tiles), axis=1)[:, :per_group]
    picked = ordered + jnp.arange(groups, dtype=jnp.int32)[:, None] * span_tiles
    return picked.reshape(-1).astype(jnp.int32)


def draw_map_one(key, part):
    return window_map(jax.random.fold_in(key, 11), PCOLS, GROUP1, WINDOW)


def draw_map_two(key, part):
    return window_map(jax.random.fold_in(key, 23), PCOLS, GROUP2, WINDOW)


def plant(values, own_key, smallest, largest):
    place = [jax.random.randint(jax.random.fold_in(own_key, axis), (), 0, length) for axis, length in enumerate(values.shape)]
    widest = values.shape.index(max(values.shape))
    beside = place[:widest] + [(place[widest] + 1) % values.shape[widest]] + place[widest + 1:]
    return values.at[tuple(place)].set(smallest).at[tuple(beside)].set(largest)


def strengthened(drawn, key, source, target, blocks, factor):
    def block_of(position):
        return (jnp.arange(drawn.shape[position]) // (drawn.shape[position] // blocks)).reshape((-1,) + (1,) * (drawn.ndim - 1 - position))

    one_side = jax.random.permutation(key, blocks)[block_of(target)]
    second = (block_of(target) + blocks // 2) % blocks
    return jnp.where((block_of(source) == one_side) | (block_of(source) == second), factor * drawn, drawn)


def level_of(rng, extent, shards, least, top_value):
    def one(axis_at, parts):
        draws = jax.random.uniform(jax.random.fold_in(jax.random.fold_in(rng, 6), axis_at), (parts,), jnp.float32, least / len(shards), top_value / len(shards))
        return jnp.repeat(jnp.exp(draws), extent[axis_at] // parts).reshape((-1,) + (1,) * (len(extent) - axis_at - 1))

    factor_of = one(*shards[0])
    for cut in shards[1:]:
        factor_of = factor_of * one(*cut)
    return factor_of


def normal_values(stream_key, shape, width, limit, split=(), kind=jnp.bfloat16):
    array = width * jax.random.normal(stream_key, shape, jnp.float32)
    if split:
        array = array * level_of(stream_key, shape, split, -0.22, 0.18)
    return jnp.clip(array, -limit, limit).astype(kind)


def noise_with(stream_key, shape, spread, bound, pieces, heavy, held_as=jnp.bfloat16):
    array = spread * jax.random.normal(stream_key, shape, jnp.float32)
    if pieces:
        array = array * level_of(stream_key, shape, pieces, -0.22, 0.18)
    return jnp.clip(strengthened(array, jax.random.fold_in(stream_key, 3), *heavy), -bound, bound).astype(held_as)


def setup_inputs(seed: int = 0) -> dict:
    arg_keys = jax.random.split(jax.random.key(seed), 6)
    updates = normal_values(arg_keys[0], (PROWS, PCOLS, GROUP1 * TILE, SLOTS * TILE), N1 ** -0.5, 0.0390625, ((0, 8), (1, 16)))
    map_one = draw_map_one(jax.random.fold_in(arg_keys[5], 71), 0)
    map_two = draw_map_two(jax.random.fold_in(arg_keys[5], 71), 0)
    seeds = plant(jax.random.randint(arg_keys[3], (PARTILES,), 0, 1073741824), jax.random.fold_in(arg_keys[3], 1), 0, 1073741823).astype(jnp.int32)
    lower = noise_with(arg_keys[4], (PCOLS, PCOLS, BORDTILES // PCOLS, TILE, (PIVTILES // PCOLS) * TILE), NPIV ** -0.5, 0.09375, ((0, 16), (3, 8)), (0, 1, 16, 2.0))
    return dict(updates=updates, map_one=map_one, map_two=map_two, seeds=seeds, lower=lower)


def mix_bits(hashed):
    hashed = hashed ^ lax.shift_right_logical(hashed, jnp.full_like(hashed, 16))
    hashed = hashed * 73244475
    hashed = hashed ^ lax.shift_right_logical(hashed, jnp.full_like(hashed, 16))
    hashed = hashed * 73244475
    hashed = hashed ^ lax.shift_right_logical(hashed, jnp.full_like(hashed, 16))
    return hashed


def sample_block(seed_rows, tile_rows, sample_count):
    offsets = jnp.arange(tile_rows, dtype=jnp.int32)[:, None] * sample_count + jnp.arange(sample_count, dtype=jnp.int32)[None, :]
    hashed = mix_bits(seed_rows.astype(jnp.int32)[:, None, None] + offsets[None])
    levels = (hashed & 65535).astype(jnp.float32)
    return ((levels - 32767.5) / 18918.6).reshape(-1, sample_count)


def rounded(values):
    return lax.optimization_barrier(values.astype(jnp.bfloat16)).astype(jnp.float32)


def reference(updates, map_one, map_two, seeds, lower):
    omega_full = sample_block(seeds, TILE, SAMPLES).astype(jnp.bfloat16).reshape(PARTILES, TILE, SAMPLES)
    parent = jnp.zeros((PARTILES, TILE, SAMPLES), jnp.float32)
    children = ((map_one, ROWS_ONE, 0, GROUP1, SLOTS1, T1TILES), (map_two, ROWS_TWO, ROWS_ONE, GROUP2, SLOTS2, T2TILES))
    for mapping, sub_rows, first_row, group, slot_total, tile_total in children:
        running = jnp.zeros((PCOLS * group * TILE, SAMPLES), jnp.float32)
        for block_index in range(sub_rows):
            places = jnp.arange(slot_total, dtype=jnp.int32) * sub_rows + block_index
            valid = places < tile_total
            clipped = jnp.minimum(places, tile_total - 1).astype(jnp.int32)
            chosen = omega_full[mapping[clipped]]
            chosen = jnp.where(valid[:, None, None], chosen, jnp.zeros_like(chosen)).reshape(slot_total * TILE, SAMPLES)
            matrix = updates[first_row + block_index][:, :group * TILE, :slot_total * TILE].reshape(PCOLS * group * TILE, slot_total * TILE)
            product = jnp.dot(matrix, chosen, preferred_element_type=jnp.float32)
            running = running + rounded(product)
        parent = parent.at[mapping].add(running.reshape(-1, TILE, SAMPLES))
    pivot_rows = parent[:PIVTILES].astype(jnp.bfloat16).reshape(PIVTILES // PCOLS, PCOLS, TILE, SAMPLES)
    border_sums = jnp.zeros((PCOLS, BORDTILES // PCOLS, TILE, SAMPLES), jnp.float32)
    for column in range(PCOLS):
        operand = pivot_rows[:, column].reshape(-1, SAMPLES)
        product = jnp.dot(lower[column].reshape(-1, operand.shape[0]), operand, preferred_element_type=jnp.float32)
        border_sums = border_sums + rounded(product).reshape(border_sums.shape)
    border = parent[PIVTILES:].reshape(BORDTILES // PCOLS, PCOLS, TILE, SAMPLES).transpose(1, 0, 2, 3)
    return border - border_sums
```

```python
import jax
import jax.numpy as jnp
from jax import lax
from jax.experimental import pallas as pl
from jax.experimental.pallas import tpu as pltpu
from jax.sharding import PartitionSpec as P

TILE = 128
SAMPLES = 1024
ROWS_ONE = 5
ROWS_TWO = 3
GROUP1 = 10
GROUP2 = 7
SLOTS1 = 32
SLOTS2 = 38
T1TILES = 160
T2TILES = 112
WINDOW = 14
PIVTILES = 64
PIVOWN = 4
SLICE = 16
KB = 256
NB = 256
HALF = 80


f32 = jnp.float32
bf16 = jnp.bfloat16


def hashed_levels(h):
    h = h ^ lax.shift_right_logical(h, jnp.full_like(h, 16))
    h = h * 73244475
    h = h ^ lax.shift_right_logical(h, jnp.full_like(h, 16))
    h = h * 73244475
    h = h ^ lax.shift_right_logical(h, jnp.full_like(h, 16))
    return ((h & 65535).astype(f32) - 32767.5) * (1.0 / 18918.6)


def child_kernel(width, start):
    steps = SLOTS2 * TILE // KB
    per = KB // TILE

    def body(where, map_one, map_two, seeds, a_ref, own_ref, other_ref, acc, omega, place_of):
        k = pl.program_id(0)
        row = where[0]
        col = where[1]
        first = row < ROWS_ONE
        my_x = row // 2
        my_core = row % 2
        live = jnp.where(first, SLOTS1 * TILE // KB, steps)

        def make(step, slot, n):
            for q in range(per):
                l = step * per + q
                p1 = jnp.minimum(l * ROWS_ONE + row, T1TILES - 1)
                p2 = l * ROWS_TWO + row - ROWS_ONE
                ok = first | (p2 < T2TILES)
                p2 = jnp.clip(p2, 0, T2TILES - 1)
                target = jnp.where(first, map_one[p1], map_two[p2])
                seed = seeds[target] + (start + n * NB)
                scale = jnp.where(ok, 1.0, 0.0).astype(f32)
                shape = (TILE, NB)
                base = lax.broadcasted_iota(jnp.int32, shape, 0) * SAMPLES + lax.broadcasted_iota(
                    jnp.int32, shape, 1
                )
                val = hashed_levels(base + seed) * scale
                omega[slot, pl.ds(q * TILE, TILE), pl.ds(pl.multiple_of(n * NB, NB), NB)] = val.astype(
                    bf16
                )

        @pl.when(k == 0)
        def _():
            acc[...] = jnp.zeros_like(acc)

            def prime(n, carry):
                make(0, 0, n)
                return carry

            lax.fori_loop(0, width // NB, prime, 0)

        @pl.when(k < live)
        def _():
            slot = k % 2

            def one(n, carry):
                make(k + 1, 1 - slot, n)
                lanes = pl.ds(pl.multiple_of(n * NB, NB), NB)
                rhs = omega[slot, :, lanes]
                low = GROUP2 * TILE
                acc[:low, lanes] += jnp.dot(a_ref[:low, :], rhs, preferred_element_type=f32)

                @pl.when(first)
                def _():
                    acc[low:, lanes] += jnp.dot(a_ref[low:, :], rhs, preferred_element_type=f32)

                return carry

            lax.fori_loop(0, width // NB, one, 0)

        @pl.when(k == steps - 1)
        def _():
            for w in range(WINDOW):
                place_of[w] = -1
            count = jnp.where(first, GROUP1, GROUP2)

            def fill(t, carry):
                i1 = jnp.minimum(col * GROUP1 + t, T1TILES - 1)
                i2 = jnp.minimum(col * GROUP2 + t, T2TILES - 1)
                w = jnp.where(first, map_one[i1], map_two[i2]) - col * WINDOW
                place_of[jnp.clip(w, 0, WINDOW - 1)] = t
                return carry

            lax.fori_loop(0, count, fill, 0)

            def emit(w, carry):
                t = place_of[w]

                @pl.when(t < 0)
                def _():
                    for rx in range(4):
                        own_ref[rx, w] = jnp.zeros((SLICE, width), bf16)
                        other_ref[rx, w] = jnp.zeros((SLICE, width), bf16)

                @pl.when(t >= 0)
                def _():
                    for rx in range(4):
                        x = (my_x + rx) % 4
                        for ref, core in ((own_ref, my_core), (other_ref, 1 - my_core)):
                            at = pl.multiple_of(t * TILE + (x * 2 + core) * SLICE, SLICE)
                            ref[rx, w] = acc[pl.ds(at, SLICE), :].astype(bf16)

                return carry

            lax.fori_loop(0, WINDOW, emit, 0)

    def a_map(k, where, *_):
        live = jnp.where(where[0] < ROWS_ONE, SLOTS1 * TILE // KB, steps)
        return (0, jnp.minimum(k, live - 1))

    shape = (4, WINDOW, SLICE, width)
    return pl.pallas_call(
        body,
        out_shape=(jax.ShapeDtypeStruct(shape, bf16), jax.ShapeDtypeStruct(shape, bf16)),
        grid_spec=pltpu.PrefetchScalarGridSpec(
            num_scalar_prefetch=4,
            grid=(steps,),
            in_specs=[pl.BlockSpec((GROUP1 * TILE, KB), a_map)],
            out_specs=[pl.BlockSpec(shape, lambda k, *_: (0, 0, 0, 0))] * 2,
            scratch_shapes=[
                pltpu.VMEM((GROUP1 * TILE, width), f32),
                pltpu.VMEM((2, KB, width), bf16),
                pltpu.SMEM((WINDOW,), jnp.int32),
            ],
        ),
        compiler_params=pltpu.CompilerParams(vmem_limit_bytes=48 << 20),
        name=f"child_{start}",
    )


def border_kernel(width):
    def body(where, low_ref, window, *refs):
        pieces = refs[:8]
        outs = refs[8:24]
        piv, prod = refs[24:]
        step = pl.program_id(0)
        row = where[0]
        col = where[1]
        my_x = row // 2
        my_core = row % 2
        my_z = col // 4
        my_y = col % 4

        @pl.when(step == 0)
        def _():
            for c in range(2):
                for rx in range(4):
                    x = (my_x + rx) % 4
                    core = my_core if c == 0 else 1 - my_core
                    for u in range(PIVOWN):
                        at = pl.multiple_of(u * TILE + (x * 2 + core) * SLICE, SLICE)
                        piv[pl.ds(at, SLICE), :] = pieces[c * 4 + rx][u]

        def one(ry, carry):
            y = (my_y + ry) % 4
            prod[ry] = -jnp.dot(low_ref[0, y], piv[...], preferred_element_type=f32)
            return carry

        lax.fori_loop(0, 4, one, 0)

        def add(o, carry):
            tile = col * WINDOW + o - PIVTILES
            owner = tile % 16
            at = pl.multiple_of((tile // 16) * SLICE, SLICE)
            z = owner // 4
            ry = (owner % 4 + 4 - my_y) % 4

            @pl.when((tile >= 0) & (z == (my_z + step) % 4))
            def _():
                prod[ry, pl.ds(at, SLICE), :] += window[o].astype(f32)

            return carry

        lax.fori_loop(0, WINDOW, add, 0)
        for rz in range(4):

            @pl.when(step == rz)
            def _():
                for ry in range(4):
                    outs[rz * 2 + ry // 2][ry % 2] = prod[ry, :HALF, :].astype(bf16)
                    outs[8 + ry * 2 + rz // 2][rz % 2] = prod[ry, HALF:, :].astype(bf16)

    whole = lambda shape: pl.BlockSpec(shape, lambda k, *_: (0,) * len(shape))
    out = (2, HALF, width)
    return pl.pallas_call(
        body,
        out_shape=[jax.ShapeDtypeStruct(out, bf16)] * 16,
        grid_spec=pltpu.PrefetchScalarGridSpec(
            num_scalar_prefetch=1,
            grid=(4,),
            in_specs=[
                pl.BlockSpec(
                    (1, 4, 2 * HALF, PIVOWN * TILE),
                    lambda k, where: ((where[1] // 4 + k) % 4, 0, 0, 0),
                ),
                whole((WINDOW, SLICE, width)),
            ]
            + [whole((PIVOWN, SLICE, width))] * 8,
            out_specs=[whole(out)] * 16,
            scratch_shapes=[
                pltpu.VMEM((PIVOWN * TILE, width), bf16),
                pltpu.VMEM((4, 2 * HALF, width), f32),
            ],
        ),
        compiler_params=pltpu.CompilerParams(vmem_limit_bytes=48 << 20),
        name="border",
    )


def along_col(value, dz, dy):
    pairs = [(z * 4 + y, ((z + dz) % 4) * 4 + (y + dy) % 4) for z in range(4) for y in range(4)]
    return lax.ppermute(value, "col", pairs)


def along_row(value, dx, dc):
    pairs = [(x * 2 + c, ((x + dx) % 4) * 2 + (c + dc) % 2) for x in range(4) for c in range(2)]
    return lax.ppermute(value, "row", pairs)


def shift_x(value, k):
    return along_row(value, k, 0)


def shift_y(value, k):
    return along_col(value, 0, k)


def shift_z(value, k):
    return along_col(value, k, 0)


def total(*values):
    result = values[0].astype(f32)
    for value in values[1:]:
        result = result + value.astype(f32)
    return result


def direct(shift, chunks):
    far = shift(chunks[2], 2)
    right = shift(chunks[1], 1)
    left = shift(chunks[3], -1)
    return total(chunks[0], right, left, far)


def ring(shift, c0, c1, c2, c3):
    relay_right = shift(c2[0], 1)
    relay_left = shift(c2[1], -1)
    early_right = shift(c1[1], 1)
    early_left = shift(c3[0], -1)
    late_right = shift(total(c1[0], relay_right).astype(bf16), 1)
    late_left = shift(total(c3[1], relay_left).astype(bf16), -1)
    return total(c0[0], early_left, late_right), total(c0[1], early_right, late_left)


def samples_block(width, start, where, updates, map_one, map_two, seeds, lower):
    col = where[1]
    own, other = child_kernel(width, start)(where, map_one, map_two, seeds, updates)
    other = along_row(other, 0, 1)
    chunks = [total(own[k], other[k]).astype(bf16) for k in range(4)]
    window = direct(shift_x, chunks).astype(bf16)
    padded = jnp.concatenate([window, jnp.zeros((2, SLICE, width), bf16), window], axis=0)
    blocks = lax.dynamic_slice_in_dim(padded, (2 * col) % 16, 16, axis=0)
    arrived = lax.all_to_all(blocks, "col", split_axis=0, concat_axis=0, tiled=True)
    mine = jnp.concatenate(
        [
            lax.dynamic_slice_in_dim(arrived, (16 * u + col) // WINDOW, 1, axis=0)
            for u in range(PIVOWN)
        ],
        axis=0,
    )
    near = [mine, shift_x(mine, -1), shift_x(mine, 2), shift_x(mine, 1)]
    far = [along_row(piece, 0, 1) for piece in near]
    outs = border_kernel(width)(where, lower, window, *near, *far)
    pairs = [outs[2 * i : 2 * i + 2] for i in range(8)]
    a0, a1 = ring(shift_z, *pairs[:4])
    b0, b1 = ring(shift_y, *pairs[4:])
    a0, a1, b0, b1 = [v.astype(bf16) for v in (a0, a1, b0, b1)]
    upper = direct(shift_y, [a0[0], a0[1], a1[0], a1[1]])
    under = direct(shift_z, [b0[0], b0[1], b1[0], b1[1]])
    return jnp.concatenate([upper, under], axis=0).reshape(1, 10, SLICE, width)


def on_device(updates, map_one, map_two, seeds, lower):
    where = jnp.stack([lax.axis_index("row"), lax.axis_index("col")]).astype(jnp.int32)
    lower = lower.reshape(4, 4, 2 * HALF, PIVOWN * TILE)
    updates = updates.reshape(updates.shape[2:])
    return samples_block(SAMPLES, 0, where, updates, map_one, map_two, seeds, lower)


def solution(mesh):
    in_specs = (P("row", "col", None, None), P(), P(), P(), P("col", None, None, "row", None))
    out_specs = P("col", None, "row", None)
    return jax.shard_map(
        on_device, mesh=mesh, in_specs=in_specs, out_specs=out_specs, check_vma=False
    )
```

```python
import jax
import jax.numpy as jnp
from jax import lax
from jax.experimental import pallas as pl
from jax.experimental.pallas import tpu as pltpu
from jax.sharding import PartitionSpec as P

TILE = 128
SAMPLES = 1024
ROWS_ONE = 5
ROWS_TWO = 3
GROUP1 = 10
GROUP2 = 7
SLOTS1 = 32
SLOTS2 = 38
T1TILES = 160
T2TILES = 112
WINDOW = 14
PIVTILES = 64
PIVOWN = 4
SLICE = 16
KB = 256
GENROWS = 16
GENLANES = 512
MPART = 128
NPART = 256
HALF = 80


f32 = jnp.float32
bf16 = jnp.bfloat16


def centred_levels(h):
    h = h ^ lax.shift_right_logical(h, jnp.full_like(h, 16))
    h = h * 73244475
    h = h ^ lax.shift_right_logical(h, jnp.full_like(h, 16))
    h = h * 73244475
    h = h ^ lax.shift_right_logical(h, jnp.full_like(h, 16))
    return (h & 65535).astype(f32) - 32767.5


def child_kernel(width, start):
    blocks_one = SLOTS1 * TILE // KB
    blocks_two = SLOTS2 * TILE // KB
    steps = (blocks_two + 1) // 2
    per = KB // TILE

    def body(where, map_one, map_two, seeds, a_ref, own_ref, other_ref, acc, even, odd, base, place_of):
        k = pl.program_id(0)
        row = where[0]
        col = where[1]
        first = row < ROWS_ONE
        my_x = row // 2
        my_core = row % 2
        live = jnp.where(first, blocks_one, blocks_two)

        def pieces(block, omega):
            for q in range(per):
                l = block * per + q
                p1 = jnp.minimum(l * ROWS_ONE + row, T1TILES - 1)
                p2 = jnp.clip(l * ROWS_TWO + row - ROWS_ONE, 0, T2TILES - 1)
                seed = seeds[jnp.where(first, map_one[p1], map_two[p2])]
                for i in range(0, TILE, GENROWS):
                    for j in range(0, width, GENLANES):
                        lanes = slice(j, j + GENLANES)
                        hashed = base[i : i + GENROWS, lanes] + seed
                        omega[q * TILE + i : q * TILE + i + GENROWS, lanes] = centred_levels(
                            hashed
                        ).astype(bf16)
                        yield

        def make(block, omega):
            for _ in pieces(block, omega):
                pass

        def clear_tail(block, omega):
            for q in range(per):
                l = block * per + q

                @pl.when(jnp.logical_not(first) & (l * ROWS_TWO + row - ROWS_ONE >= T2TILES))
                def _():
                    omega[q * TILE : (q + 1) * TILE, :] = jnp.zeros((TILE, width), bf16)

        @pl.when(k == 0)
        def _():
            acc[...] = jnp.zeros_like(acc)
            base[...] = (
                lax.broadcasted_iota(jnp.int32, (TILE, width), 0) * SAMPLES
                + lax.broadcasted_iota(jnp.int32, (TILE, width), 1)
                + start
            )
            make(0, even)

        def substep(half, now, coming):
            block = 2 * k + half
            lanes = slice(half * KB, (half + 1) * KB)
            clear_tail(block, now)
            for mine, rows in ((first, GROUP1 * TILE), (jnp.logical_not(first), GROUP2 * TILE)):

                @pl.when(mine & (block < live))
                def _():
                    work = pieces(block + 1, coming)
                    parts = rows // MPART
                    dots = parts * (width // NPART)
                    share = (KB // GENROWS) * (width // GENLANES) / dots
                    done = 0
                    for n in range(width // NPART):
                        cols = slice(n * NPART, (n + 1) * NPART)
                        for m in range(parts):
                            part = slice(m * MPART, (m + 1) * MPART)
                            acc[part, cols] += jnp.dot(
                                a_ref[part, lanes], now[:, cols], preferred_element_type=f32
                            )
                            want = round((n * parts + m + 1) * share)
                            while done < want:
                                next(work)
                                done += 1

        substep(0, even, odd)
        substep(1, odd, even)

        @pl.when(k == steps - 1)
        def _():
            for w in range(WINDOW):
                place_of[w] = -1
            count = jnp.where(first, GROUP1, GROUP2)

            def fill(t, carry):
                i1 = jnp.minimum(col * GROUP1 + t, T1TILES - 1)
                i2 = jnp.minimum(col * GROUP2 + t, T2TILES - 1)
                w = jnp.where(first, map_one[i1], map_two[i2]) - col * WINDOW
                place_of[jnp.clip(w, 0, WINDOW - 1)] = t
                return carry

            lax.fori_loop(0, count, fill, 0)

            def emit(w, carry):
                t = place_of[w]

                @pl.when(t < 0)
                def _():
                    for rx in range(4):
                        own_ref[rx, w] = jnp.zeros((SLICE, width), bf16)
                        other_ref[rx, w] = jnp.zeros((SLICE, width), bf16)

                @pl.when(t >= 0)
                def _():
                    for rx in range(4):
                        x = (my_x + rx) % 4
                        for ref, core in ((own_ref, my_core), (other_ref, 1 - my_core)):
                            at = pl.multiple_of(t * TILE + (x * 2 + core) * SLICE, SLICE)
                            ref[rx, w] = (acc[pl.ds(at, SLICE), :] * (1.0 / 18918.6)).astype(bf16)

                return carry

            lax.fori_loop(0, WINDOW, emit, 0)

    def a_map(k, where, *_):
        live = jnp.where(where[0] < ROWS_ONE, blocks_one // 2, steps)
        return (0, jnp.minimum(k, live - 1))

    shape = (4, WINDOW, SLICE, width)
    return pl.pallas_call(
        body,
        out_shape=(jax.ShapeDtypeStruct(shape, bf16), jax.ShapeDtypeStruct(shape, bf16)),
        grid_spec=pltpu.PrefetchScalarGridSpec(
            num_scalar_prefetch=4,
            grid=(steps,),
            in_specs=[pl.BlockSpec((GROUP1 * TILE, 2 * KB), a_map)],
            out_specs=[pl.BlockSpec(shape, lambda k, *_: (0, 0, 0, 0))] * 2,
            scratch_shapes=[
                pltpu.VMEM((GROUP1 * TILE, width), f32),
                pltpu.VMEM((KB, width), bf16),
                pltpu.VMEM((KB, width), bf16),
                pltpu.VMEM((TILE, width), jnp.int32),
                pltpu.SMEM((WINDOW,), jnp.int32),
            ],
        ),
        compiler_params=pltpu.CompilerParams(vmem_limit_bytes=48 << 20),
        name=f"child_{start}",
    )


def border_kernel(width):
    def body(where, low_ref, window, *refs):
        pieces = refs[:8]
        outs = refs[8:24]
        piv, prod = refs[24:]
        step = pl.program_id(0)
        row = where[0]
        col = where[1]
        my_x = row // 2
        my_core = row % 2
        my_z = col // 4
        my_y = col % 4

        @pl.when(step == 0)
        def _():
            for c in range(2):
                for rx in range(4):
                    x = (my_x + rx) % 4
                    core = my_core if c == 0 else 1 - my_core
                    for u in range(PIVOWN):
                        at = pl.multiple_of(u * TILE + (x * 2 + core) * SLICE, SLICE)
                        piv[pl.ds(at, SLICE), :] = pieces[c * 4 + rx][u]

        prod[...] = jnp.dot(low_ref[0], piv[...], preferred_element_type=f32)

        def add(o, carry):
            tile = col * WINDOW + o - PIVTILES
            owner = tile % 16
            at = pl.multiple_of((owner % 4) * (2 * HALF) + (tile // 16) * SLICE, SLICE)
            z = owner // 4

            @pl.when((tile >= 0) & (z == (my_z + step) % 4))
            def _():
                prod[pl.ds(at, SLICE), :] -= window[o].astype(f32)

            return carry

        lax.fori_loop(0, WINDOW, add, 0)
        for rz in range(4):

            @pl.when(step == rz)
            def _():
                for ry in range(4):
                    at = pl.multiple_of((my_y + ry) % 4 * (2 * HALF), SLICE)
                    upper = prod[pl.ds(at, HALF), :]
                    under = prod[pl.ds(pl.multiple_of(at + HALF, SLICE), HALF), :]
                    outs[rz * 2 + ry // 2][ry % 2] = (-upper).astype(bf16)
                    outs[8 + ry * 2 + rz // 2][rz % 2] = (-under).astype(bf16)

    whole = lambda shape: pl.BlockSpec(shape, lambda k, *_: (0,) * len(shape))
    out = (2, HALF, width)
    return pl.pallas_call(
        body,
        out_shape=[jax.ShapeDtypeStruct(out, bf16)] * 16,
        grid_spec=pltpu.PrefetchScalarGridSpec(
            num_scalar_prefetch=1,
            grid=(4,),
            in_specs=[
                pl.BlockSpec(
                    (1, 8 * HALF, PIVOWN * TILE),
                    lambda k, where: ((where[1] // 4 + k) % 4, 0, 0),
                ),
                whole((WINDOW, SLICE, width)),
            ]
            + [whole((PIVOWN, SLICE, width))] * 8,
            out_specs=[whole(out)] * 16,
            scratch_shapes=[
                pltpu.VMEM((PIVOWN * TILE, width), bf16),
                pltpu.VMEM((8 * HALF, width), f32),
            ],
        ),
        compiler_params=pltpu.CompilerParams(vmem_limit_bytes=48 << 20),
        name="border",
    )


def along_col(value, dz, dy):
    pairs = [(z * 4 + y, ((z + dz) % 4) * 4 + (y + dy) % 4) for z in range(4) for y in range(4)]
    return lax.ppermute(value, "col", pairs)


def along_row(value, dx, dc):
    pairs = [(x * 2 + c, ((x + dx) % 4) * 2 + (c + dc) % 2) for x in range(4) for c in range(2)]
    return lax.ppermute(value, "row", pairs)


def shift_x(value, k):
    return along_row(value, k, 0)


def shift_y(value, k):
    return along_col(value, 0, k)


def shift_z(value, k):
    return along_col(value, k, 0)


def total(*values):
    result = values[0].astype(f32)
    for value in values[1:]:
        result = result + value.astype(f32)
    return result


def direct(shift, chunks):
    far = shift(chunks[2], 2)
    right = shift(chunks[1], 1)
    left = shift(chunks[3], -1)
    return total(chunks[0], right, left, far)


def ring(shift, c0, c1, c2, c3):
    relay_right = shift(c2[0], 1)
    relay_left = shift(c2[1], -1)
    early_right = shift(c1[1], 1)
    early_left = shift(c3[0], -1)
    late_right = shift(total(c1[0], relay_right).astype(bf16), 1)
    late_left = shift(total(c3[1], relay_left).astype(bf16), -1)
    return total(c0[0], early_left, late_right), total(c0[1], early_right, late_left)


def samples_block(width, start, where, updates, map_one, map_two, seeds, lower):
    col = where[1]
    own, other = child_kernel(width, start)(where, map_one, map_two, seeds, updates)
    other = along_row(other, 0, 1)
    chunks = [total(own[k], other[k]).astype(bf16) for k in range(4)]
    window = direct(shift_x, chunks).astype(bf16)
    padded = jnp.concatenate([window, jnp.zeros((2, SLICE, width), bf16), window], axis=0)
    blocks = lax.dynamic_slice_in_dim(padded, (2 * col) % 16, 16, axis=0)
    arrived = lax.all_to_all(blocks, "col", split_axis=0, concat_axis=0, tiled=True)
    mine = jnp.concatenate(
        [
            lax.dynamic_slice_in_dim(arrived, (16 * u + col) // WINDOW, 1, axis=0)
            for u in range(PIVOWN)
        ],
        axis=0,
    )
    near = [mine, shift_x(mine, -1), shift_x(mine, 2), shift_x(mine, 1)]
    far = [along_row(piece, 0, 1) for piece in near]
    outs = border_kernel(width)(where, lower, window, *near, *far)
    pairs = [outs[2 * i : 2 * i + 2] for i in range(8)]
    a0, a1 = ring(shift_z, *pairs[:4])
    b0, b1 = ring(shift_y, *pairs[4:])
    a0, a1, b0, b1 = [v.astype(bf16) for v in (a0, a1, b0, b1)]
    upper = direct(shift_y, [a0[0], a0[1], a1[0], a1[1]])
    under = direct(shift_z, [b0[0], b0[1], b1[0], b1[1]])
    return jnp.concatenate([upper, under], axis=0).reshape(1, 10, SLICE, width)


def on_device(updates, map_one, map_two, seeds, lower):
    where = jnp.stack([lax.axis_index("row"), lax.axis_index("col")]).astype(jnp.int32)
    lower = lower.reshape(4, 8 * HALF, PIVOWN * TILE)
    updates = updates.reshape(updates.shape[2:])
    return samples_block(SAMPLES, 0, where, updates, map_one, map_two, seeds, lower)


def solution(mesh):
    in_specs = (P("row", "col", None, None), P(), P(), P(), P("col", None, None, "row", None))
    out_specs = P("col", None, "row", None)
    return jax.shard_map(
        on_device, mesh=mesh, in_specs=in_specs, out_specs=out_specs, check_vma=False
    )
```

```python
import jax
import jax.numpy as jnp
from jax import lax
from jax.experimental import pallas as pl
from jax.experimental.pallas import tpu as pltpu
from jax.sharding import PartitionSpec as P

TILE = 128
SAMPLES = 1024
ROWS_ONE = 5
ROWS_TWO = 3
GROUP1 = 10
GROUP2 = 7
SLOTS1 = 32
SLOTS2 = 38
T1TILES = 160
T2TILES = 112
WINDOW = 14
PIVTILES = 64
PIVOWN = 4
SLICE = 16
KB = 512
GENROWS = 16
GENLANES = 512
PARTS = 2
NPART = 256
HALF = 80


f32 = jnp.float32
bf16 = jnp.bfloat16


def centred_levels(h):
    h = h ^ lax.shift_right_logical(h, jnp.full_like(h, 16))
    h = h * 73244475
    h = h ^ lax.shift_right_logical(h, jnp.full_like(h, 16))
    h = h * 73244475
    h = h ^ lax.shift_right_logical(h, jnp.full_like(h, 16))
    return (h & 65535).astype(f32) - 32767.5


def child_kernel(width, start):
    steps_one = SLOTS1 * TILE // KB
    steps = (SLOTS2 * TILE + KB - 1) // KB
    tail = SLOTS2 * TILE - (steps - 1) * KB
    per = KB // TILE

    def body(where, map_one, map_two, seeds, a_ref, own_ref, other_ref, acc, even, odd, base, place_of):
        k = pl.program_id(0)
        row = where[0]
        col = where[1]
        first = row < ROWS_ONE
        second = jnp.logical_not(first)
        my_x = row // 2
        my_core = row % 2

        def pieces(block, omega):
            for q in range(per):
                l = block * per + q
                p1 = jnp.minimum(l * ROWS_ONE + row, T1TILES - 1)
                p2 = jnp.clip(l * ROWS_TWO + row - ROWS_ONE, 0, T2TILES - 1)
                seed = seeds[jnp.where(first, map_one[p1], map_two[p2])]
                for i in range(0, TILE, GENROWS):
                    for j in range(0, width, GENLANES):
                        lanes = slice(j, j + GENLANES)
                        hashed = base[i : i + GENROWS, lanes] + seed
                        omega[q * TILE + i : q * TILE + i + GENROWS, lanes] = centred_levels(
                            hashed
                        ).astype(bf16)
                        yield

        def product(rows, depth, now, work):
            chunks = KB // GENROWS * (width // GENLANES)
            part = rows // PARTS
            dots = PARTS * (width // NPART)
            done = 0
            for n in range(width // NPART):
                cols = slice(n * NPART, (n + 1) * NPART)
                for m in range(PARTS):
                    lines = slice(m * part, (m + 1) * part)
                    acc[lines, cols] += jnp.dot(
                        a_ref[lines, :depth], now[:depth, cols], preferred_element_type=f32
                    )
                    want = (n * PARTS + m + 1) * chunks // dots
                    while work is not None and done < want:
                        next(work)
                        done += 1

        @pl.when(k == 0)
        def _():
            acc[...] = jnp.zeros_like(acc)
            base[...] = (
                lax.broadcasted_iota(jnp.int32, (TILE, width), 0) * SAMPLES
                + lax.broadcasted_iota(jnp.int32, (TILE, width), 1)
                + start
            )
            for _ in pieces(0, even):
                pass

        last = second & (k == steps - 1)
        for parity, now, coming in ((0, even, odd), (1, odd, even)):
            for mine, rows in (
                (first & (k < steps_one), GROUP1 * TILE),
                (second & (k < steps - 1), GROUP2 * TILE),
            ):

                @pl.when(mine & (k % 2 == parity))
                def _():
                    product(rows, KB, now, pieces(k + 1, coming))

        now = odd if (steps - 1) % 2 else even
        for q in range(tail // TILE):
            l = (steps - 1) * per + q

            @pl.when(last & (l * ROWS_TWO + row - ROWS_ONE >= T2TILES))
            def _():
                now[q * TILE : (q + 1) * TILE, :] = jnp.zeros((TILE, width), bf16)

        @pl.when(last)
        def _():
            product(GROUP2 * TILE, tail, now, None)

        @pl.when(k == steps - 1)
        def _():
            for w in range(WINDOW):
                place_of[w] = -1
            count = jnp.where(first, GROUP1, GROUP2)

            def fill(t, carry):
                i1 = jnp.minimum(col * GROUP1 + t, T1TILES - 1)
                i2 = jnp.minimum(col * GROUP2 + t, T2TILES - 1)
                w = jnp.where(first, map_one[i1], map_two[i2]) - col * WINDOW
                place_of[jnp.clip(w, 0, WINDOW - 1)] = t
                return carry

            lax.fori_loop(0, count, fill, 0)

            def emit(w, carry):
                t = place_of[w]

                @pl.when(t < 0)
                def _():
                    for rx in range(4):
                        own_ref[rx, w] = jnp.zeros((SLICE, width), bf16)
                        other_ref[rx, w] = jnp.zeros((SLICE, width), bf16)

                @pl.when(t >= 0)
                def _():
                    for rx in range(4):
                        x = (my_x + rx) % 4
                        for ref, core in ((own_ref, my_core), (other_ref, 1 - my_core)):
                            at = pl.multiple_of(t * TILE + (x * 2 + core) * SLICE, SLICE)
                            ref[rx, w] = (acc[pl.ds(at, SLICE), :] * (1.0 / 18918.6)).astype(bf16)

                return carry

            lax.fori_loop(0, WINDOW, emit, 0)

    def a_map(k, where, *_):
        live = jnp.where(where[0] < ROWS_ONE, steps_one, steps)
        return (0, jnp.minimum(k, live - 1))

    shape = (4, WINDOW, SLICE, width)
    return pl.pallas_call(
        body,
        out_shape=(jax.ShapeDtypeStruct(shape, bf16), jax.ShapeDtypeStruct(shape, bf16)),
        grid_spec=pltpu.PrefetchScalarGridSpec(
            num_scalar_prefetch=4,
            grid=(steps,),
            in_specs=[pl.BlockSpec((GROUP1 * TILE, KB), a_map)],
            out_specs=[pl.BlockSpec(shape, lambda k, *_: (0, 0, 0, 0))] * 2,
            scratch_shapes=[
                pltpu.VMEM((GROUP1 * TILE, width), f32),
                pltpu.VMEM((KB, width), bf16),
                pltpu.VMEM((KB, width), bf16),
                pltpu.VMEM((TILE, width), jnp.int32),
                pltpu.SMEM((WINDOW,), jnp.int32),
            ],
        ),
        compiler_params=pltpu.CompilerParams(vmem_limit_bytes=48 << 20),
        name=f"child_{start}",
    )


def border_kernel(width):
    def body(where, low_ref, window, *refs):
        pieces = refs[:8]
        outs = refs[8:24]
        piv, prod = refs[24:]
        step = pl.program_id(0)
        row = where[0]
        col = where[1]
        my_x = row // 2
        my_core = row % 2
        my_z = col // 4
        my_y = col % 4

        @pl.when(step == 0)
        def _():
            for c in range(2):
                for rx in range(4):
                    x = (my_x + rx) % 4
                    core = my_core if c == 0 else 1 - my_core
                    for u in range(PIVOWN):
                        at = pl.multiple_of(u * TILE + (x * 2 + core) * SLICE, SLICE)
                        piv[pl.ds(at, SLICE), :] = pieces[c * 4 + rx][u]

        prod[...] = jnp.dot(low_ref[0], piv[...], preferred_element_type=f32)

        def add(o, carry):
            tile = col * WINDOW + o - PIVTILES
            owner = tile % 16
            at = pl.multiple_of((owner % 4) * (2 * HALF) + (tile // 16) * SLICE, SLICE)
            z = owner // 4

            @pl.when((tile >= 0) & (z == (my_z + step) % 4))
            def _():
                prod[pl.ds(at, SLICE), :] -= window[o].astype(f32)

            return carry

        lax.fori_loop(0, WINDOW, add, 0)
        for rz in range(4):

            @pl.when(step == rz)
            def _():
                for ry in range(4):
                    at = pl.multiple_of((my_y + ry) % 4 * (2 * HALF), SLICE)
                    upper = prod[pl.ds(at, HALF), :]
                    under = prod[pl.ds(pl.multiple_of(at + HALF, SLICE), HALF), :]
                    outs[rz * 2 + ry // 2][ry % 2] = (-upper).astype(bf16)
                    outs[8 + ry * 2 + rz // 2][rz % 2] = (-under).astype(bf16)

    whole = lambda shape: pl.BlockSpec(shape, lambda k, *_: (0,) * len(shape))
    out = (2, HALF, width)
    return pl.pallas_call(
        body,
        out_shape=[jax.ShapeDtypeStruct(out, bf16)] * 16,
        grid_spec=pltpu.PrefetchScalarGridSpec(
            num_scalar_prefetch=1,
            grid=(4,),
            in_specs=[
                pl.BlockSpec(
                    (1, 8 * HALF, PIVOWN * TILE),
                    lambda k, where: ((where[1] // 4 + k) % 4, 0, 0),
                ),
                whole((WINDOW, SLICE, width)),
            ]
            + [whole((PIVOWN, SLICE, width))] * 8,
            out_specs=[whole(out)] * 16,
            scratch_shapes=[
                pltpu.VMEM((PIVOWN * TILE, width), bf16),
                pltpu.VMEM((8 * HALF, width), f32),
            ],
        ),
        compiler_params=pltpu.CompilerParams(vmem_limit_bytes=48 << 20),
        name="border",
    )


def along_col(value, dz, dy):
    pairs = [(z * 4 + y, ((z + dz) % 4) * 4 + (y + dy) % 4) for z in range(4) for y in range(4)]
    return lax.ppermute(value, "col", pairs)


def along_row(value, dx, dc):
    pairs = [(x * 2 + c, ((x + dx) % 4) * 2 + (c + dc) % 2) for x in range(4) for c in range(2)]
    return lax.ppermute(value, "row", pairs)


def shift_x(value, k):
    return along_row(value, k, 0)


def shift_y(value, k):
    return along_col(value, 0, k)


def shift_z(value, k):
    return along_col(value, k, 0)


def total(*values):
    result = values[0].astype(f32)
    for value in values[1:]:
        result = result + value.astype(f32)
    return result


def direct(shift, chunks):
    far = shift(chunks[2], 2)
    right = shift(chunks[1], 1)
    left = shift(chunks[3], -1)
    return total(chunks[0], right, left, far)


def ring(shift, c0, c1, c2, c3):
    relay_right = shift(c2[0], 1)
    relay_left = shift(c2[1], -1)
    early_right = shift(c1[1], 1)
    early_left = shift(c3[0], -1)
    late_right = shift(total(c1[0], relay_right).astype(bf16), 1)
    late_left = shift(total(c3[1], relay_left).astype(bf16), -1)
    return total(c0[0], early_left, late_right), total(c0[1], early_right, late_left)


def short_ring(shift, c0, c1, c2, c3):
    half = c0.shape[0] // 2
    relay_right = shift(c2[:half], 1)
    relay_left = shift(c2[half:], -1)
    right = jnp.concatenate([total(c1[:half], relay_right).astype(bf16), c1[half:]], axis=0)
    left = jnp.concatenate([c3[:half], total(c3[half:], relay_left).astype(bf16)], axis=0)
    return total(c0, shift(right, 1), shift(left, -1))


def samples_block(width, start, where, updates, map_one, map_two, seeds, lower):
    col = where[1]
    own, other = child_kernel(width, start)(where, map_one, map_two, seeds, updates)
    other = along_row(other, 0, 1)
    chunks = [total(own[k], other[k]).astype(bf16) for k in range(4)]
    window = short_ring(shift_x, *chunks).astype(bf16)
    padded = jnp.concatenate([window, jnp.zeros((2, SLICE, width), bf16), window], axis=0)
    blocks = lax.dynamic_slice_in_dim(padded, (2 * col) % 16, 16, axis=0)
    arrived = lax.all_to_all(blocks, "col", split_axis=0, concat_axis=0, tiled=True)
    mine = jnp.concatenate(
        [
            lax.dynamic_slice_in_dim(arrived, (16 * u + col) // WINDOW, 1, axis=0)
            for u in range(PIVOWN)
        ],
        axis=0,
    )
    near = [mine, shift_x(mine, -1), shift_x(mine, 2), shift_x(mine, 1)]
    far = [along_row(piece, 0, 1) for piece in near]
    outs = border_kernel(width)(where, lower, window, *near, *far)
    pairs = [outs[2 * i : 2 * i + 2] for i in range(8)]
    a0, a1 = ring(shift_z, *pairs[:4])
    b0, b1 = ring(shift_y, *pairs[4:])
    a0, a1, b0, b1 = [v.astype(bf16) for v in (a0, a1, b0, b1)]
    upper = direct(shift_y, [a0[0], a0[1], a1[0], a1[1]])
    under = direct(shift_z, [b0[0], b0[1], b1[0], b1[1]])
    return jnp.concatenate([upper, under], axis=0).reshape(1, 10, SLICE, width)


def on_device(updates, map_one, map_two, seeds, lower):
    where = jnp.stack([lax.axis_index("row"), lax.axis_index("col")]).astype(jnp.int32)
    lower = lower.reshape(4, 8 * HALF, PIVOWN * TILE)
    updates = updates.reshape(updates.shape[2:])
    return samples_block(SAMPLES, 0, where, updates, map_one, map_two, seeds, lower)


def solution(mesh):
    in_specs = (P("row", "col", None, None), P(), P(), P(), P("col", None, None, "row", None))
    out_specs = P("col", None, "row", None)
    return jax.shard_map(
        on_device, mesh=mesh, in_specs=in_specs, out_specs=out_specs, check_vma=False
    )
```

```python
import jax
import jax.numpy as jnp
from jax import lax
from jax.experimental import pallas as pl
from jax.experimental.pallas import tpu as pltpu
from jax.sharding import PartitionSpec as P

TILE = 128
SAMPLES = 1024
ROWS_ONE = 5
ROWS_TWO = 3
GROUP1 = 10
GROUP2 = 7
SLOTS1 = 32
SLOTS2 = 38
T1TILES = 160
T2TILES = 112
PARTILES = 224
WINDOW = 14
PIVTILES = 64
PIVOWN = 4
SLICE = 16
KB = 512
GENROWS = 16
GENLANES = 512
PARTS = 2
NPART = 256
HALF = 80


f32 = jnp.float32
bf16 = jnp.bfloat16


def centred_levels(h):
    h = h ^ lax.shift_right_logical(h, jnp.full_like(h, 16))
    h = h * 73244475
    h = h ^ lax.shift_right_logical(h, jnp.full_like(h, 16))
    h = h * 73244475
    h = h ^ lax.shift_right_logical(h, jnp.full_like(h, 16))
    return (h & 65535).astype(f32) - 32767.5


def child_kernel(width, start):
    steps_one = SLOTS1 * TILE // KB
    steps = (SLOTS2 * TILE + KB - 1) // KB
    tail = SLOTS2 * TILE - (steps - 1) * KB
    per = KB // TILE

    def body(where, in_one, in_two, in_seeds, a_ref, own_ref, other_ref, acc, even, odd, base, place_of, *tables):
        map_one, map_two, seeds, arrived = tables
        k = pl.program_id(0)
        row = where[0]
        col = where[1]
        first = row < ROWS_ONE
        second = jnp.logical_not(first)
        my_x = row // 2
        my_core = row % 2

        def pieces(block, omega):
            for q in range(per):
                l = block * per + q
                p1 = jnp.minimum(l * ROWS_ONE + row, T1TILES - 1)
                p2 = jnp.clip(l * ROWS_TWO + row - ROWS_ONE, 0, T2TILES - 1)
                seed = seeds[jnp.where(first, map_one[p1], map_two[p2])]
                for i in range(0, TILE, GENROWS):
                    for j in range(0, width, GENLANES):
                        lanes = slice(j, j + GENLANES)
                        hashed = base[i : i + GENROWS, lanes] + seed
                        omega[q * TILE + i : q * TILE + i + GENROWS, lanes] = centred_levels(
                            hashed
                        ).astype(bf16)
                        yield

        def product(rows, depth, now, work):
            chunks = KB // GENROWS * (width // GENLANES)
            part = rows // PARTS
            dots = PARTS * (width // NPART)
            done = 0
            for n in range(width // NPART):
                cols = slice(n * NPART, (n + 1) * NPART)
                for m in range(PARTS):
                    lines = slice(m * part, (m + 1) * part)
                    acc[lines, cols] += jnp.dot(
                        a_ref[lines, :depth], now[:depth, cols], preferred_element_type=f32
                    )
                    want = (n * PARTS + m + 1) * chunks // dots
                    while work is not None and done < want:
                        next(work)
                        done += 1

        @pl.when(k == 0)
        def _():
            loads = [
                pltpu.make_async_copy(source, table, arrived.at[i])
                for i, (source, table) in enumerate(
                    ((in_one, map_one), (in_two, map_two), (in_seeds, seeds))
                )
            ]
            for load in loads:
                load.start()
            acc[...] = jnp.zeros_like(acc)
            base[...] = (
                lax.broadcasted_iota(jnp.int32, (TILE, width), 0) * SAMPLES
                + lax.broadcasted_iota(jnp.int32, (TILE, width), 1)
                + start
            )
            for load in loads:
                load.wait()
            for _ in pieces(0, even):
                pass

        last = second & (k == steps - 1)
        for parity, now, coming in ((0, even, odd), (1, odd, even)):
            for mine, rows in (
                (first & (k < steps_one), GROUP1 * TILE),
                (second & (k < steps - 1), GROUP2 * TILE),
            ):

                @pl.when(mine & (k % 2 == parity))
                def _():
                    product(rows, KB, now, pieces(k + 1, coming))

        now = odd if (steps - 1) % 2 else even
        for q in range(tail // TILE):
            l = (steps - 1) * per + q

            @pl.when(last & (l * ROWS_TWO + row - ROWS_ONE >= T2TILES))
            def _():
                now[q * TILE : (q + 1) * TILE, :] = jnp.zeros((TILE, width), bf16)

        @pl.when(last)
        def _():
            product(GROUP2 * TILE, tail, now, None)

        @pl.when(k == steps - 1)
        def _():
            for w in range(WINDOW):
                place_of[w] = -1
            count = jnp.where(first, GROUP1, GROUP2)

            def fill(t, carry):
                i1 = jnp.minimum(col * GROUP1 + t, T1TILES - 1)
                i2 = jnp.minimum(col * GROUP2 + t, T2TILES - 1)
                w = jnp.where(first, map_one[i1], map_two[i2]) - col * WINDOW
                place_of[jnp.clip(w, 0, WINDOW - 1)] = t
                return carry

            lax.fori_loop(0, count, fill, 0)

            def emit(w, carry):
                t = place_of[w]

                @pl.when(t < 0)
                def _():
                    for rx in range(4):
                        own_ref[rx, w] = jnp.zeros((SLICE, width), bf16)
                        other_ref[rx, w] = jnp.zeros((SLICE, width), bf16)

                @pl.when(t >= 0)
                def _():
                    for rx in range(4):
                        x = (my_x + rx) % 4
                        for ref, core in ((own_ref, my_core), (other_ref, 1 - my_core)):
                            at = pl.multiple_of(t * TILE + (x * 2 + core) * SLICE, SLICE)
                            ref[rx, w] = (acc[pl.ds(at, SLICE), :] * (1.0 / 18918.6)).astype(bf16)

                return carry

            lax.fori_loop(0, WINDOW, emit, 0)

    def a_map(k, where, *_):
        live = jnp.where(where[0] < ROWS_ONE, steps_one, steps)
        return (0, jnp.minimum(k, live - 1))

    shape = (4, WINDOW, SLICE, width)
    return pl.pallas_call(
        body,
        out_shape=(jax.ShapeDtypeStruct(shape, bf16), jax.ShapeDtypeStruct(shape, bf16)),
        grid_spec=pltpu.PrefetchScalarGridSpec(
            num_scalar_prefetch=1,
            grid=(steps,),
            in_specs=[pl.BlockSpec(memory_space=pltpu.HBM)] * 3
            + [pl.BlockSpec((GROUP1 * TILE, KB), a_map)],
            out_specs=[pl.BlockSpec(shape, lambda k, *_: (0, 0, 0, 0))] * 2,
            scratch_shapes=[
                pltpu.VMEM((GROUP1 * TILE, width), f32),
                pltpu.VMEM((KB, width), bf16),
                pltpu.VMEM((KB, width), bf16),
                pltpu.VMEM((TILE, width), jnp.int32),
                pltpu.SMEM((WINDOW,), jnp.int32),
                pltpu.SMEM((T1TILES,), jnp.int32),
                pltpu.SMEM((T2TILES,), jnp.int32),
                pltpu.SMEM((PARTILES,), jnp.int32),
                pltpu.SemaphoreType.DMA((3,)),
            ],
        ),
        compiler_params=pltpu.CompilerParams(vmem_limit_bytes=26 << 20),
        name=f"child_{start}",
    )


def vmem():
    return pl.BlockSpec(memory_space=pltpu.VMEM)


def border_kernel(width):
    def body(where, low_ref, window, *refs):
        pieces = refs[:8]
        outs = refs[8:24]
        piv = refs[24]
        row = where[0]
        col = where[1]
        my_x = row // 2
        my_core = row % 2
        my_z = col // 4
        my_y = col % 4
        for c in range(2):
            for rx in range(4):
                x = (my_x + rx) % 4
                core = my_core if c == 0 else 1 - my_core
                for u in range(PIVOWN):
                    at = pl.multiple_of(u * TILE + (x * 2 + core) * SLICE, SLICE)
                    piv[pl.ds(at, SLICE), :] = pieces[c * 4 + rx][u]

        for rz in (2, 1, 3, 0):
            z = (my_z + rz) % 4
            for ry in range(4):
                at = pl.multiple_of((my_y + ry) % 4 * (2 * HALF), SLICE)
                term = -jnp.dot(
                    low_ref[z, pl.ds(at, 2 * HALF), :], piv[...], preferred_element_type=f32
                )
                outs[rz * 2 + ry // 2][ry % 2] = term[:HALF].astype(bf16)
                outs[8 + ry * 2 + rz // 2][rz % 2] = term[HALF:].astype(bf16)

        def add(o, carry):
            tile = col * WINDOW + o - PIVTILES
            owner = tile % 16
            t = tile // 16
            rz = (owner // 4 + 4 - my_z) % 4
            ry = (owner % 4 + 4 - my_y) % 4

            def into(ref, lead, at):
                rows = pl.ds(pl.multiple_of(at, SLICE), SLICE)
                ref[lead, rows, :] = (ref[lead, rows, :].astype(f32) + window[o].astype(f32)).astype(bf16)

            @pl.when((tile >= 0) & (t < 5))
            def _():
                for i in range(8):

                    @pl.when(rz * 2 + ry // 2 == i)
                    def _():
                        into(outs[i], ry % 2, t * SLICE)

            @pl.when((tile >= 0) & (t >= 5))
            def _():
                for i in range(8):

                    @pl.when(ry * 2 + rz // 2 == i)
                    def _():
                        into(outs[8 + i], rz % 2, (t - 5) * SLICE)

            return carry

        lax.fori_loop(0, WINDOW, add, 0)

    return pl.pallas_call(
        body,
        out_shape=[jax.ShapeDtypeStruct((2, HALF, width), bf16)] * 16,
        in_specs=[pl.BlockSpec(memory_space=pltpu.SMEM)] + [vmem()] * 10,
        out_specs=[vmem()] * 16,
        scratch_shapes=[pltpu.VMEM((PIVOWN * TILE, width), bf16)],
        compiler_params=pltpu.CompilerParams(vmem_limit_bytes=12 << 20),
        name="border",
    )


def window_kernel(width):
    def body(where, mine, right, left, window, blocks):
        col = where[1]
        for o in range(16):
            place = (col * WINDOW + o) % 16
            if o < WINDOW:
                value = mine[o].astype(f32) + right[o].astype(f32) + left[o].astype(f32)
                window[o] = value.astype(bf16)
                blocks[place] = value.astype(bf16)
            else:
                blocks[place] = jnp.zeros((SLICE, width), bf16)

    return pl.pallas_call(
        body,
        out_shape=[
            jax.ShapeDtypeStruct((WINDOW, SLICE, width), bf16),
            jax.ShapeDtypeStruct((16, SLICE, width), bf16),
        ],
        in_specs=[pl.BlockSpec(memory_space=pltpu.SMEM)] + [vmem()] * 3,
        out_specs=[vmem()] * 2,
        compiler_params=pltpu.CompilerParams(vmem_limit_bytes=4 << 20),
        name="window",
    )


def along_col(value, dz, dy):
    pairs = [(z * 4 + y, ((z + dz) % 4) * 4 + (y + dy) % 4) for z in range(4) for y in range(4)]
    return lax.ppermute(value, "col", pairs)


def along_row(value, dx, dc):
    pairs = [(x * 2 + c, ((x + dx) % 4) * 2 + (c + dc) % 2) for x in range(4) for c in range(2)]
    return lax.ppermute(value, "row", pairs)


def shift_x(value, k):
    return along_row(value, k, 0)


def shift_y(value, k):
    return along_col(value, 0, k)


def shift_z(value, k):
    return along_col(value, k, 0)


def total(*values):
    result = values[0].astype(f32)
    for value in values[1:]:
        result = result + value.astype(f32)
    return result


def direct(shift, chunks):
    far = shift(chunks[2], 2)
    right = shift(chunks[1], 1)
    left = shift(chunks[3], -1)
    return total(chunks[0], right, left, far)


def ring(shift, c0, c1, c2, c3):
    relay_right = shift(c2[0], 1)
    relay_left = shift(c2[1], -1)
    early_right = shift(c1[1], 1)
    early_left = shift(c3[0], -1)
    late_right = shift(total(c1[0], relay_right).astype(bf16), 1)
    late_left = shift(total(c3[1], relay_left).astype(bf16), -1)
    return total(c0[0], early_left, late_right), total(c0[1], early_right, late_left)


def short_ring(shift, c0, c1, c2, c3):
    half = c0.shape[0] // 2
    relay_right = shift(c2[:half], 1)
    relay_left = shift(c2[half:], -1)
    right = jnp.concatenate([total(c1[:half], relay_right).astype(bf16), c1[half:]], axis=0)
    left = jnp.concatenate([c3[:half], total(c3[half:], relay_left).astype(bf16)], axis=0)
    return c0, shift(right, 1), shift(left, -1)


def samples_block(width, start, where, updates, map_one, map_two, seeds, lower):
    col = where[1]
    own, other = child_kernel(width, start)(where, map_one, map_two, seeds, updates)
    other = along_row(other, 0, 1)
    chunks = [total(own[k], other[k]).astype(bf16) for k in range(4)]
    window, blocks = window_kernel(width)(where, *short_ring(shift_x, *chunks))
    arrived = lax.all_to_all(blocks, "col", split_axis=0, concat_axis=0, tiled=True)
    mine = jnp.concatenate(
        [
            lax.dynamic_slice_in_dim(arrived, (16 * u + col) // WINDOW, 1, axis=0)
            for u in range(PIVOWN)
        ],
        axis=0,
    )
    near = [mine, shift_x(mine, -1), shift_x(mine, 2), shift_x(mine, 1)]
    far = [along_row(piece, 0, 1) for piece in near]
    outs = border_kernel(width)(where, lower, window, *near, *far)
    pairs = [outs[2 * i : 2 * i + 2] for i in range(8)]
    a0, a1 = ring(shift_z, *pairs[:4])
    b0, b1 = ring(shift_y, *pairs[4:])
    a0, a1, b0, b1 = [v.astype(bf16) for v in (a0, a1, b0, b1)]
    upper = direct(shift_y, [a0[0], a0[1], a1[0], a1[1]])
    under = direct(shift_z, [b0[0], b0[1], b1[0], b1[1]])
    return jnp.concatenate([upper, under], axis=0).reshape(1, 10, SLICE, width)


def on_device(updates, map_one, map_two, seeds, lower):
    updates, map_one, map_two, seeds = [
        pltpu.with_memory_space_constraint(v, pltpu.HBM)
        for v in (updates.reshape(updates.shape[2:]), map_one, map_two, seeds)
    ]
    where = jnp.stack([lax.axis_index("row"), lax.axis_index("col")]).astype(jnp.int32)
    lower = lower.reshape(4, 8 * HALF, PIVOWN * TILE)
    return samples_block(SAMPLES, 0, where, updates, map_one, map_two, seeds, lower)


def solution(mesh):
    in_specs = (P("row", "col", None, None), P(), P(), P(), P("col", None, None, "row", None))
    out_specs = P("col", None, "row", None)
    return jax.shard_map(
        on_device, mesh=mesh, in_specs=in_specs, out_specs=out_specs, check_vma=False
    )
```
